32 devices in a mesh: dp: 8 (over z, y), tensor: 4 (over x, core).
Axes of the slice: x: 2, y: 2, z: 4, core: 2. Of those that a mesh axis runs over, the one named last changes fastest.
Arguments:
- tree_ids: int32 [8, 64], P('dp'), may hold values from 0 to 65535, as said below
- ancestors: int32 [8, 64, 64], P('dp'), may hold values from 0 to 1, as said below
- lengths: int32 [8], P('dp'), may hold values from 64 to 1024, as said below
- table: bfloat16 [65536, 4096], P('dp', 'tensor'), may hold values from -3 to 3
- gain: bfloat16 [4096], replicated, may hold values from 0.25 to 1.75
- w_query: bfloat16 [4096, 4096], P(None, 'tensor'), may hold values from -0.09375 to 0.09375
- w_kv: bfloat16 [2, 4096, 1024], P(None, None, 'tensor'), may hold values from -0.09375 to 0.09375
- w_out: bfloat16 [4096, 4096], P('tensor'), may hold values from -0.09375 to 0.09375
- key_cache: bfloat16 [8, 8, 1024, 128], P('dp', 'tensor'), may hold values from -480 to 480
- value_cache: bfloat16 [8, 8, 1024, 128], P('dp', 'tensor'), may hold values from -6 to 6
Outputs:
- layer_output: bfloat16 [512, 4096], P('dp', 'tensor')
The draws below stay inside these ranges and needn't reach their ends.
Inputs may be any that keep to these rules, and one draw needn't show every extreme that they name: `tree_ids`: split the vocabulary into equal consecutive parts, one for each index of dp; of the nodes of the rows of one index of dp, at most 16 have ids in any one part, and exactly 16 in some part. Row n of each row's matrix marks node n and all its ancestors in that row's tree; node 0 is the root and every other node's parent has a smaller index. `lengths`: some row has all 1024 slots live.
All inputs are finite; a program needn't handle non-finite values.
Results may differ from the reference program's by a relative error of at most 0.004.
The reference program's roundings to bfloat16 on the way count: a program that leaves them out, or rounds other values in their place, can miss the bound.
Values may be sent and summed in bfloat16 or wider, within the bound.
A program may use at most 128 MiB of HBM per device.

```python
import math
import jax
import jax.numpy as jnp
from jax import lax

D = 4096
HEADS = 32
KVH = 8
HD = 128
VOCAB = 65536
NODES = 64
CTX = 1024
R_DEV = 1
ROWS = 8
TOKENS = 512
CAP = 16
N_DP = 8


def draw_tree_ids(key, part):
    block_size = R_DEV * NODES
    part_rows = VOCAB // N_DP
    block_keys = jax.random.split(key, N_DP)

    def one_block(block_key):
        chosen_key, order_key, place_key, entry_key = jax.random.split(block_key, 4)
        chosen = jax.random.randint(chosen_key, (), 0, N_DP)
        others_index = jnp.arange(CAP * (N_DP - 1), dtype=jnp.int32) // CAP
        others_owner = others_index + (others_index >= chosen).astype(jnp.int32)
        others_owner = jax.random.permutation(order_key, others_owner)
        owners_all = jnp.concatenate([jnp.full((CAP,), chosen, jnp.int32), others_owner])
        owners_block = jax.random.permutation(place_key, owners_all[:block_size])
        entries = jax.random.randint(entry_key, (block_size,), 0, part_rows)
        return (owners_block * part_rows + entries).astype(jnp.int32)
    drawn = jax.vmap(one_block)(block_keys)
    return drawn.reshape(ROWS, NODES).astype(jnp.int32)


def draw_ancestors(key, part):
    raw_bits = jax.random.randint(key, (ROWS, NODES), 0, 2 ** 30)
    node_index = jnp.arange(NODES, dtype=jnp.int32)
    parents = raw_bits % jnp.maximum(node_index, 1)[None, :]

    def build(parent_row):
        start_matrix = jnp.zeros((NODES, NODES), jnp.int32).at[0, 0].set(1)

        def add_node(node, matrix):
            new_row = matrix[parent_row[node]].at[node].set(1)
            return matrix.at[node].set(new_row)
        return lax.fori_loop(1, NODES, add_node, start_matrix)
    return jax.vmap(build)(parents).astype(jnp.int32)


def draw_lengths(key, part):
    first_key, second_key = jax.random.split(key)
    values_drawn = jax.random.randint(first_key, (ROWS,), CTX // 16, CTX + 1)
    chosen = jax.random.randint(second_key, (), 0, ROWS)
    return jnp.where(jnp.arange(ROWS) == chosen, CTX, values_drawn).astype(jnp.int32)


def draw_key_cache(key, part):
    base_draw = jnp.clip(jax.random.normal(key, (ROWS, KVH, CTX, HD), jnp.float32), -8.0, 8.0) * 2.5
    return base_draw.astype(jnp.bfloat16)


def levels(stream_key, shape, cuts, smallest, high):
    level, own = 1.0, jax.random.fold_in(stream_key, 6)
    for position, parts in cuts:
        heights = jnp.exp(jax.random.uniform(jax.random.fold_in(own, position), (parts,), jnp.float32, smallest / len(cuts), high / len(cuts)))
        level = level * jnp.repeat(heights, shape[position] // parts).reshape([-1 if axis == position else 1 for axis in range(len(shape))])
    return level


def normal_values(key, extent, scale, limit, cuts=(), held_as=jnp.bfloat16):
    level = levels(key, extent, cuts, -0.22, 0.18) if cuts else 1.0
    array = jax.random.normal(key, extent, jnp.float32) * scale * level
    return jnp.minimum(jnp.maximum(array, -limit), limit).astype(held_as)


def setup_inputs(seed: int = 0) -> dict:
    seeds = jax.random.split(jax.random.key(seed), 11)
    return {
        "tree_ids": draw_tree_ids(jax.random.fold_in(seeds[10], 71), 0),
        "ancestors": draw_ancestors(jax.random.fold_in(seeds[10], 71), 0),
        "lengths": draw_lengths(jax.random.fold_in(seeds[10], 71), 0),
        "table": normal_values(seeds[3], (VOCAB, D), 0.5, 3.0, ((0, 8), (1, 4))),
        "gain": jnp.clip(1.0 + 0.15 * jax.random.normal(seeds[4], (D,), jnp.float32), 0.25, 1.75).astype(jnp.bfloat16),
        "w_query": normal_values(seeds[5], (D, HEADS * HD), D ** -0.5, 0.09375, ((1, 4),)),
        "w_kv": normal_values(seeds[6], (2, D, KVH * HD), D ** -0.5, 0.09375, ((2, 4),)),
        "w_out": normal_values(seeds[7], (HEADS * HD, D), (HEADS * HD) ** -0.5, 0.09375, ((0, 4),)),
        "key_cache": draw_key_cache(jax.random.fold_in(seeds[10], 71), 0),
        "value_cache": normal_values(seeds[9], (ROWS, KVH, CTX, HD), 1.0, 6.0, ((0, 8), (1, 4))),
    }


EPS = 1e-05
NEG = -1e+30
THETA = 500000.0

def rotary(values, positions):
    half_dim = values.shape[-1] // 2
    freq_index = jnp.arange(half_dim, dtype=jnp.float32)
    inverse = jnp.exp(freq_index * (-2.0 * math.log(THETA) / values.shape[-1]))
    angles = positions[:, None] * inverse[None, :]
    cosine = jnp.cos(angles)[:, None, :]
    sine_part = jnp.sin(angles)[:, None, :]
    lower_half = values[..., :half_dim]
    upper_half = values[..., half_dim:]
    return jnp.concatenate([lower_half * cosine - upper_half * sine_part, upper_half * cosine + lower_half * sine_part], axis=-1)

def contract(left_side, right_side):
    return lax.dot_general(left_side, right_side, (((1,), (1,)), ((), ())), preferred_element_type=jnp.float32)

def attend(query_group, keys_tree, values_tree, keys_cache, values_cache, live_len, tree_mask):
    score_scale = keys_cache.shape[-1] ** (-0.5)
    cache_scores = contract(query_group, keys_cache) * score_scale
    columns = jnp.arange(keys_cache.shape[0], dtype=jnp.int32)
    cache_scores = jnp.where(columns[None, :] < live_len, cache_scores, NEG)
    tree_scores = contract(query_group, keys_tree) * score_scale
    groups = query_group.shape[0] // tree_mask.shape[0]
    tree_scores = jnp.where(jnp.tile(tree_mask, (groups, 1)) > 0, tree_scores, NEG)
    row_top = jnp.maximum(lax.optimization_barrier(jnp.max(cache_scores, axis=1)), lax.optimization_barrier(jnp.max(tree_scores, axis=1)))[:, None]
    cache_exp = jnp.exp(cache_scores - row_top)
    tree_exp = jnp.exp(tree_scores - row_top)
    denominator = lax.optimization_barrier(jnp.sum(cache_exp, axis=1)) + lax.optimization_barrier(jnp.sum(tree_exp, axis=1))
    weighted = jnp.dot(cache_exp.astype(jnp.bfloat16), values_cache, preferred_element_type=jnp.float32)
    weighted = weighted + jnp.dot(tree_exp.astype(jnp.bfloat16), values_tree, preferred_element_type=jnp.float32)
    return (weighted / denominator[:, None]).astype(jnp.bfloat16)

def to_groups(tensor_in, kv_heads, head_dim):
    row_count, node_count, width_all = tensor_in.shape
    per_group = width_all // (kv_heads * head_dim)
    grouped = tensor_in.reshape(row_count, node_count, kv_heads, per_group, head_dim).transpose(0, 2, 3, 1, 4)
    return grouped.reshape(row_count, kv_heads, per_group * node_count, head_dim)

def from_groups(tensor_in, node_count):
    row_count, kv_heads, group_rows, head_dim = tensor_in.shape
    grouped = tensor_in.reshape(row_count, kv_heads, group_rows // node_count, node_count, head_dim)
    return grouped.transpose(0, 3, 1, 2, 4).reshape(row_count, node_count, -1)

def reference(tree_ids, ancestors, lengths, table, gain, w_query, w_kv, w_out, key_cache, value_cache):
    embedded = table[tree_ids.reshape(-1)]
    features = embedded.astype(jnp.float32)
    inv_rms = lax.rsqrt(lax.optimization_barrier(jnp.sum(features * features, axis=1)) / D + EPS)
    normed = (features * inv_rms[:, None] * gain.astype(jnp.float32)[None, :]).astype(jnp.bfloat16)
    queries = jnp.dot(normed, w_query, preferred_element_type=jnp.float32)
    keys_new = jnp.dot(normed, w_kv[0], preferred_element_type=jnp.float32)
    values_new = jnp.dot(normed, w_kv[1], preferred_element_type=jnp.float32).astype(jnp.bfloat16)
    node_depth = lax.optimization_barrier(jnp.sum(ancestors, axis=2)) - 1
    positions = (lengths[:, None] + node_depth).reshape(-1).astype(jnp.float32)
    queries = rotary(queries.reshape(TOKENS, HEADS, HD), positions).astype(jnp.bfloat16).reshape(ROWS, NODES, HEADS * HD)
    keys_new = rotary(keys_new.reshape(TOKENS, KVH, HD), positions).astype(jnp.bfloat16).reshape(ROWS, NODES, KVH * HD)
    values_new = values_new.reshape(ROWS, NODES, KVH * HD)
    query_groups = to_groups(queries, KVH, HD)
    key_groups = to_groups(keys_new, KVH, HD)
    value_groups = to_groups(values_new, KVH, HD)

    def per_row(row_items):
        row_q, row_k, row_v, row_kc, row_vc, live_len, tree_mask = row_items

        def per_head(head_items):
            return attend(head_items[0], head_items[1], head_items[2], head_items[3], head_items[4], live_len, tree_mask)
        return lax.map(per_head, (row_q, row_k, row_v, row_kc, row_vc))
    contexts = lax.map(per_row, (query_groups, key_groups, value_groups, key_cache, value_cache, lengths, ancestors))
    contexts = from_groups(contexts, NODES).reshape(TOKENS, HEADS * HD)
    attention = jnp.dot(contexts, w_out, preferred_element_type=jnp.float32)
    return (features + attention).astype(jnp.bfloat16)
```

```python
import functools
import math

import jax
import jax.numpy as jnp
from jax import lax
from jax.experimental import pallas as pl
from jax.experimental.pallas import tpu as pltpu
from jax.sharding import PartitionSpec as P

EPS = 1e-05
NEG = -1e30
THETA = 500000.0
MESH = pl.DeviceIdType.MESH


def layer_kernel(
    n_dp,
    n_t,
    capacity,
    ids_hbm,
    anc_hbm,
    len_hbm,
    gain_hbm,
    table_hbm,
    wq_hbm,
    wkv_hbm,
    wout_hbm,
    kc_hbm,
    vc_hbm,
    out_ref,
    ids_v,
    codes_v,
    codes_s,
    anc_v,
    len_s,
    gain_v,
    cos_v,
    sin_v,
    place_v,
    table_v,
    group_v,
    wq_v,
    wkv_v,
    wout_v,
    kc_v,
    vc_v,
    slot_send,
    slot_recv,
    ss_send,
    ss_recv,
    sst_send,
    sst_recv,
    emb_all,
    ctx_v,
    rs1_send,
    rs1_recv,
    rs2_send,
    rs2_recv,
    small_sem,
    table_sem,
    w_sem,
    wout_sem,
    ids_ssem,
    ids_rsem,
    row_ssem,
    row_rsem,
    ss_ssem,
    ss_rsem,
    sst_ssem,
    sst_rsem,
    ag_ssem,
    ag_rsem,
    fw_ssem,
    rs1_ssem,
    rs1_rsem,
    rs2_ssem,
    rs2_rsem,
):
    me = lax.axis_index("dp")
    t = lax.axis_index("tensor")
    chip = t // 2
    parity = t % 2
    partner = t + 1 - 2 * parity
    n_chip = n_t // 2
    nodes = ids_v.shape[-1]
    tiles, tile, width = table_v.shape
    vocab_rows = tiles * tile
    head_dim = kc_v.shape[-1]
    kv_local = kc_v.shape[0]
    heads = wq_v.shape[1] // head_dim
    groups = heads // kv_local
    slots = n_dp * capacity
    span = 4 * capacity * tile
    absent = 2 * capacity * tile
    n_part = emb_all.shape[0]
    part_width = width // n_part
    n_rs = rs1_send.shape[1]
    rs_width = width // n_rs

    def peer(m):
        return lax.rem(me + m, n_dp)

    def back(m):
        return (n_dp - m) % n_dp

    others = list(range(1, n_dp))

    barrier = pltpu.get_barrier_semaphore()
    for m in others:
        pl.semaphore_signal(barrier, inc=1, device_id={"dp": peer(m)}, device_id_type=MESH)
    for k in range(1, n_t):
        pl.semaphore_signal(
            barrier, inc=1, device_id={"tensor": lax.rem(t + k, n_t)}, device_id_type=MESH
        )
    small_copies = [
        pltpu.make_async_copy(ids_hbm, ids_v, small_sem.at[0]),
        pltpu.make_async_copy(anc_hbm.at[0], anc_v, small_sem.at[1]),
        pltpu.make_async_copy(len_hbm, len_s, small_sem.at[2]),
        pltpu.make_async_copy(gain_hbm, gain_v, small_sem.at[3]),
    ]
    for copy in small_copies:
        copy.start()
    n_tab = table_sem.shape[0]
    tab_step = tiles // n_tab
    table_copies = [
        pltpu.make_async_copy(
            table_hbm.at[pl.ds(i * tab_step, tab_step)],
            table_v.at[pl.ds(i * tab_step, tab_step)],
            table_sem.at[i],
        )
        for i in range(n_tab)
    ]
    for copy in table_copies:
        copy.start()
    small_copies[0].wait()
    sub = lax.broadcasted_iota(jnp.int32, (nodes, nodes), 0)
    lane = lax.broadcasted_iota(jnp.int32, (nodes, nodes), 1)
    ids_row = ids_v[...]
    ids = jnp.sum(jnp.where(sub == lane, ids_row, 0), axis=1, keepdims=True)
    owner = ids // vocab_rows
    alike = (owner == ids_row // vocab_rows) & (lane < sub)
    rank = jnp.sum(jnp.where(alike, 1, 0), axis=1, keepdims=True)
    node_slot = lax.rem(owner - me + n_dp, n_dp) * capacity + rank
    slot_index = lax.broadcasted_iota(jnp.int32, (nodes, slots), 1)
    placed = (node_slot == slot_index) & (rank < capacity)
    place_v[...] = jnp.where(placed, 1.0, 0.0)
    offset = ids - owner * vocab_rows
    code = (offset // tile) * span + lax.rem(offset, tile)
    codes_v[...] = jnp.sum(jnp.where(placed, code - absent, 0), axis=0, keepdims=True) + absent
    own_codes = pltpu.make_async_copy(codes_v, codes_s.at[0], small_sem.at[4])
    own_codes.start()
    pl.semaphore_wait(barrier, n_dp + n_t - 2)

    def dp_copy(src, dst, ssem, rsem, m):
        return pltpu.make_async_remote_copy(
            src_ref=src,
            dst_ref=dst,
            send_sem=ssem,
            recv_sem=rsem,
            device_id={"dp": peer(m)},
            device_id_type=MESH,
        )

    def t_copy(src, dst, ssem, rsem, target):
        return pltpu.make_async_remote_copy(
            src_ref=src,
            dst_ref=dst,
            send_sem=ssem,
            recv_sem=rsem,
            device_id={"tensor": target},
            device_id_type=MESH,
        )

    ids_copies = [
        dp_copy(codes_v, codes_s.at[back(m)], ids_ssem.at[m], ids_rsem.at[back(m)], m)
        for m in others
    ]
    for copy in ids_copies:
        copy.start()

    for copy in small_copies[1:]:
        copy.wait()
    live_slots = len_s[0]
    depth = jnp.sum(anc_v[...].astype(jnp.float32), axis=1, keepdims=True)
    positions = depth + (live_slots - 1).astype(jnp.float32)
    half_dim = head_dim // 2
    lanes = lax.broadcasted_iota(jnp.int32, (1, head_dim), 1)
    freq_index = jnp.where(lanes < half_dim, lanes, lanes - half_dim).astype(jnp.float32)
    angles = positions * jnp.exp(freq_index * (-2.0 * math.log(THETA) / head_dim))
    cosine = jnp.cos(angles)
    sine = jnp.where(lanes < half_dim, -jnp.sin(angles), jnp.sin(angles))
    cos_v[...] = cosine
    sin_v[...] = sine

    for copy in table_copies:
        copy.wait()

    w_copies = [
        pltpu.make_async_copy(wq_hbm, wq_v, w_sem.at[0]),
        pltpu.make_async_copy(wkv_hbm, wkv_v, w_sem.at[1]),
        pltpu.make_async_copy(kc_hbm.at[0], kc_v, w_sem.at[2]),
        pltpu.make_async_copy(vc_hbm.at[0], vc_v, w_sem.at[3]),
    ]
    wout_copies = []
    for k in list(range(1, n_chip)) + [0]:
        target_chip = lax.rem(chip + k, n_chip)
        for which in range(2):
            chunk = 2 * target_chip + (parity if which else 1 - parity)
            start = pl.multiple_of(chunk * width, width)
            wout_copies.append(
                pltpu.make_async_copy(
                    wout_hbm.at[:, pl.ds(start, width)],
                    wout_v.at[2 * k + which],
                    wout_sem.at[2 * k + which],
                )
            )
    for copy in w_copies + wout_copies:
        copy.start()

    own_codes.wait()
    for copy in ids_copies:
        copy.wait_recv()
    row_copies = []
    ss_copies = []
    block_sub = lax.broadcasted_iota(jnp.int32, (capacity, 128), 0)
    block_lane = lax.broadcasted_iota(jnp.int32, (capacity, 128), 1)
    squares = [None] * n_dp

    def send_row(q, m):
        copy = dp_copy(
            slot_send.at[q, m],
            slot_recv.at[q, back(m)],
            row_ssem.at[q, m],
            row_rsem.at[q, back(m)],
            m,
        )
        copy.start()
        row_copies.append(copy)

    for m in others + [0]:
        target = jnp.full((capacity, 128), -1, jnp.int32)
        for i in range(capacity):
            code = codes_s[m, 0, back(m) * capacity + i]
            group = lax.div(code, span)
            row = (m * capacity + i) * tile
            group_v[row : row + tile, :] = table_v[group]
            target = jnp.where(block_sub == i, i * tile + code - group * span, target)
        pick = jnp.concatenate(
            [
                (block_lane + h == target).astype(jnp.float32).astype(jnp.bfloat16)
                for h in range(0, capacity * tile, 128)
            ],
            axis=1,
        )
        start = m * capacity * tile
        rows = jnp.dot(
            pick,
            group_v[start : start + capacity * tile, :],
            preferred_element_type=jnp.float32,
        )
        squares[m] = jnp.sum(rows * rows, axis=1, keepdims=True)
        for q in range(n_part):
            packed = rows[:, q * part_width : (q + 1) * part_width].astype(jnp.bfloat16)
            if m:
                slot_send[q, m] = packed
            else:
                slot_recv[q, 0] = packed
        if m:
            send_row(0, m)
    ordered = jnp.concatenate([squares[back(m)] for m in range(n_dp)], axis=0)
    row = jnp.broadcast_to(ordered, (slots, 128)).T[0:1]
    ss_send[...] = row
    ss_recv[0] = row
    for m in others:
        copy = dp_copy(ss_send, ss_recv.at[back(m)], ss_ssem.at[m], ss_rsem.at[back(m)], m)
        copy.start()
        ss_copies.append(copy)
    for q in range(1, n_part):
        for m in others:
            send_row(q, m)

    def ag_copy(q, origin, ssem, target):
        return t_copy(
            emb_all.at[q, origin], emb_all.at[q, origin], ssem, ag_rsem.at[q, origin], target
        )

    ag_copies = []
    fw_copies = []
    sst_copies = []

    def forward(q):
        for k in range(1, n_chip):
            origin = lax.rem(t - 2 * k + n_t, n_t)
            copy = ag_copy(q, origin, fw_ssem.at[q, k], partner)
            copy.wait_recv()
            copy.start()
            fw_copies.append(copy)

    def gathered(q):
        ag_copy(q, partner, ag_ssem.at[q, 0], partner).wait_recv()
        for k in range(1, n_chip):
            origin = lax.rem(partner - 2 * k + n_t, n_t)
            ag_copy(q, origin, ag_ssem.at[q, 0], partner).wait_recv()

    place = place_v[...].astype(jnp.bfloat16)
    slot_lane = lax.broadcasted_iota(jnp.int32, (1, slots), 1) // capacity
    for q in range(n_part):
        if q == n_part - 1:
            row = jnp.zeros((1, slots), jnp.float32)
            for m in range(n_dp):
                if m:
                    dp_copy(ss_send, ss_recv.at[m], ss_ssem.at[m], ss_rsem.at[m], m).wait_recv()
                row = jnp.where(slot_lane == m, ss_recv[m], row)
            sst_send[...] = row
            for k in range(1, n_t):
                copy = t_copy(
                    sst_send,
                    sst_recv.at[n_t - k],
                    sst_ssem.at[k],
                    sst_rsem.at[n_t - k],
                    lax.rem(t + k, n_t),
                )
                copy.start()
                sst_copies.append(copy)
        for m in range(1, n_dp):
            dp_copy(
                slot_send.at[q, m], slot_recv.at[q, m], row_ssem.at[q, m], row_rsem.at[q, m], m
            ).wait_recv()
        embedded = jnp.dot(
            place, slot_recv[q].reshape(slots, part_width), preferred_element_type=jnp.float32
        )
        emb_all[q, t] = embedded.astype(jnp.bfloat16)
        for k in list(range(1, n_chip)) + [0]:
            copy = ag_copy(q, t, ag_ssem.at[q, k], lax.rem(t + 2 * k, n_t) if k else partner)
            copy.start()
            ag_copies.append(copy)
        if q:
            forward(q - 1)

    total_row = sst_send[...]
    for k in range(1, n_t):
        t_copy(sst_send, sst_recv.at[k], sst_ssem.at[k], sst_rsem.at[k], partner).wait_recv()
        total_row = total_row + sst_recv[k]
    node_squares = jnp.sum(place_v[...] * total_row, axis=1, keepdims=True)
    inv_rms = lax.rsqrt(node_squares / (n_t * width) + EPS)
    for copy in w_copies:
        copy.wait()

    def project(first, last, sums):
        queries, keys, values = sums
        for j in range(n_t):
            start = j * width + first * part_width
            span = slice(start, start + (last - first) * part_width)
            gain = gain_v[span].astype(jnp.float32)[None, :]
            parts = [emb_all[q, j] for q in range(first, last)]
            features = jnp.concatenate(parts, axis=1) if len(parts) > 1 else parts[0]
            normed = (features.astype(jnp.float32) * inv_rms * gain).astype(jnp.bfloat16)
            queries = queries + jnp.dot(
                normed, wq_v[span, :], preferred_element_type=jnp.float32
            )
            keys = keys + jnp.dot(normed, wkv_v[0, span, :], preferred_element_type=jnp.float32)
            values = values + jnp.dot(
                normed, wkv_v[1, span, :], preferred_element_type=jnp.float32
            )
        return queries, keys, values

    sums = (
        jnp.zeros((nodes, wq_v.shape[1]), jnp.float32),
        jnp.zeros((nodes, wkv_v.shape[2]), jnp.float32),
        jnp.zeros((nodes, wkv_v.shape[2]), jnp.float32),
    )
    if n_part > 1:
        for q in range(n_part - 1):
            gathered(q)
        sums = project(0, n_part - 1, sums)
    forward(n_part - 1)
    gathered(n_part - 1)
    queries, keys_raw, values_raw = project(n_part - 1, n_part, sums)
    values_new = values_raw.astype(jnp.bfloat16)
    cosine = cos_v[...]
    sine = sin_v[...]

    def rotary(values):
        return (values * cosine + pltpu.roll(values, head_dim // 2, 1) * sine).astype(jnp.bfloat16)

    scale = head_dim ** (-0.5)
    live = lax.broadcasted_iota(jnp.int32, (1, kc_v.shape[1]), 1) < live_slots
    tree = jnp.concatenate([anc_v[...]] * groups, axis=0) > 0
    contract = (((1,), (1,)), ((), ()))
    for kv in range(kv_local):
        cols = slice(kv * head_dim, (kv + 1) * head_dim)
        query = jnp.concatenate(
            [
                rotary(queries[:, h * head_dim : (h + 1) * head_dim])
                for h in range(kv * groups, (kv + 1) * groups)
            ],
            axis=0,
        )
        key_tree = rotary(keys_raw[:, cols])
        cache_scores = (
            lax.dot_general(query, kc_v[kv], contract, preferred_element_type=jnp.float32) * scale
        )
        cache_scores = jnp.where(live, cache_scores, NEG)
        tree_scores = (
            lax.dot_general(query, key_tree, contract, preferred_element_type=jnp.float32) * scale
        )
        tree_scores = jnp.where(tree, tree_scores, NEG)
        top = jnp.maximum(
            jnp.max(cache_scores, axis=1, keepdims=True),
            jnp.max(tree_scores, axis=1, keepdims=True),
        )
        cache_exp = jnp.exp(cache_scores - top)
        tree_exp = jnp.exp(tree_scores - top)
        denominator = jnp.sum(cache_exp, axis=1, keepdims=True) + jnp.sum(
            tree_exp, axis=1, keepdims=True
        )
        weighted = jnp.dot(
            tree_exp.astype(jnp.bfloat16), values_new[:, cols], preferred_element_type=jnp.float32
        ) + jnp.dot(cache_exp.astype(jnp.bfloat16), vc_v[kv], preferred_element_type=jnp.float32)
        context = (weighted / denominator).astype(jnp.bfloat16)
        for g in range(groups):
            h = kv * groups + g
            ctx_v[:, h * head_dim : (h + 1) * head_dim] = context[g * nodes : (g + 1) * nodes]

    for copy in wout_copies:
        copy.wait()
    contexts = ctx_v[...]
    rs1_copies = {}
    rs2_copies = {}

    half = contexts.shape[1] // 2

    def out_part(block, c):
        cols = slice(c * rs_width, (c + 1) * rs_width)
        return jnp.dot(
            contexts[:, :half], wout_v[block, :half, cols], preferred_element_type=jnp.float32
        ) + jnp.dot(
            contexts[:, half:], wout_v[block, half:, cols], preferred_element_type=jnp.float32
        )

    def to_partner(k):
        for c in range(n_rs):
            rs1_send[k, c] = out_part(2 * k, c).astype(jnp.bfloat16)
            rs1_copies[k, c] = t_copy(
                rs1_send.at[k, c], rs1_recv.at[k, c], rs1_ssem.at[k, c], rs1_rsem.at[k, c], partner
            )
            rs1_copies[k, c].start()

    for k in range(1, n_chip):
        to_partner(k)
    for k in range(1, n_chip):
        for c in range(n_rs):
            part = out_part(2 * k + 1, c)
            rs1_copies[k, c].wait_recv()
            rs2_send[k, c] = (part + rs1_recv[k, c].astype(jnp.float32)).astype(jnp.bfloat16)
            rs2_copies[k, c] = t_copy(
                rs2_send.at[k, c],
                rs2_recv.at[k, c],
                rs2_ssem.at[k, c],
                rs2_rsem.at[k, c],
                lax.rem(t + 2 * k, n_t),
            )
            rs2_copies[k, c].start()
    to_partner(0)
    own = jnp.concatenate([emb_all[q, t].astype(jnp.float32) for q in range(n_part)], axis=1)
    sums = []
    for c in range(n_rs):
        part = out_part(1, c)
        rs1_copies[0, c].wait_recv()
        part = part + rs1_recv[0, c].astype(jnp.float32)
        sums.append(part + own[:, c * rs_width : (c + 1) * rs_width])
    for c in range(n_rs):
        total = sums[c]
        for k in range(1, n_chip):
            rs2_copies[k, c].wait_recv()
            total = total + rs2_recv[k, c].astype(jnp.float32)
        out_ref[:, c * rs_width : (c + 1) * rs_width] = total.astype(out_ref.dtype)
    for copy in (
        ids_copies
        + row_copies
        + ss_copies
        + ag_copies
        + sst_copies
        + fw_copies
        + list(rs1_copies.values())
        + list(rs2_copies.values())
    ):
        copy.wait_send()


def shards(tree_ids, ancestors, lengths, table, gain, w_query, w_kv, w_out, key_cache, value_cache):
    n_dp = lax.axis_size("dp")
    n_t = lax.axis_size("tensor")
    n_chip = n_t // 2
    row_count, nodes = tree_ids.shape
    vocab_rows, width = table.shape
    head_dim = key_cache.shape[3]
    capacity = 2 * ((row_count * nodes + n_dp - 1) // n_dp)
    capacity = 16 * ((capacity + 15) // 16)
    bf16, f32 = jnp.bfloat16, jnp.float32
    n_tab = 4
    tile = 16
    n_part = 2
    n_rs = 2
    part_width = width // n_part
    rs_width = width // n_rs
    slots = n_dp * capacity
    sems = pltpu.SemaphoreType.DMA
    hbm = pl.BlockSpec(memory_space=pl.ANY)
    return pl.pallas_call(
        functools.partial(layer_kernel, n_dp, n_t, capacity),
        out_shape=jax.ShapeDtypeStruct((nodes, width), bf16),
        in_specs=[hbm] * 2 + [pl.BlockSpec(memory_space=pltpu.HBM)] + [hbm] * 7,
        out_specs=pl.BlockSpec(memory_space=pltpu.VMEM),
        scratch_shapes=[
            pltpu.VMEM((1, nodes), jnp.int32),
            pltpu.VMEM((1, slots), jnp.int32),
            pltpu.SMEM((n_dp, 1, slots), jnp.int32),
            pltpu.VMEM((nodes, nodes), jnp.int32),
            pltpu.SMEM(lengths.shape, jnp.int32),
            pltpu.VMEM(gain.shape, bf16),
            pltpu.VMEM((nodes, head_dim), f32),
            pltpu.VMEM((nodes, head_dim), f32),
            pltpu.VMEM((nodes, slots), f32),
            pltpu.VMEM((vocab_rows // tile, tile, width), bf16),
            pltpu.VMEM((slots * tile, width), bf16),
            pltpu.VMEM(w_query.shape, bf16),
            pltpu.VMEM(w_kv.shape, bf16),
            pltpu.VMEM((n_t, w_out.shape[0], width), bf16),
            pltpu.VMEM(key_cache.shape[1:], bf16),
            pltpu.VMEM(value_cache.shape[1:], bf16),
            pltpu.VMEM((n_part, n_dp, capacity, part_width), bf16),
            pltpu.VMEM((n_part, n_dp, capacity, part_width), bf16),
            pltpu.VMEM((1, slots), f32),
            pltpu.VMEM((n_dp, 1, slots), f32),
            pltpu.VMEM((1, slots), f32),
            pltpu.VMEM((n_t, 1, slots), f32),
            pltpu.VMEM((n_part, n_t, nodes, part_width), bf16),
            pltpu.VMEM((nodes, w_query.shape[1]), bf16),
            pltpu.VMEM((n_chip, n_rs, nodes, rs_width), bf16),
            pltpu.VMEM((n_chip, n_rs, nodes, rs_width), bf16),
            pltpu.VMEM((n_chip, n_rs, nodes, rs_width), bf16),
            pltpu.VMEM((n_chip, n_rs, nodes, rs_width), bf16),
            sems((5,)),
            sems((n_tab,)),
            sems((4,)),
            sems((n_t,)),
            sems((n_dp,)),
            sems((n_dp,)),
            sems((n_part, n_dp)),
            sems((n_part, n_dp)),
            sems((n_dp,)),
            sems((n_dp,)),
            sems((n_t,)),
            sems((n_t,)),
            sems((n_part, n_chip)),
            sems((n_part, n_t)),
            sems((n_part, n_chip)),
            sems((n_chip, n_rs)),
            sems((n_chip, n_rs)),
            sems((n_chip, n_rs)),
            sems((n_chip, n_rs)),
        ],
        compiler_params=pltpu.CompilerParams(
            collective_id=0, has_side_effects=True, vmem_limit_bytes=62 * 1024 * 1024
        ),
    )(
        tree_ids,
        ancestors,
        lengths,
        gain,
        table.reshape(vocab_rows // tile, tile, width),
        w_query,
        w_kv,
        w_out,
        key_cache,
        value_cache,
    )


def solution(mesh):
    in_specs = (
        P("dp", None),
        P("dp", None, None),
        P("dp"),
        P("dp", "tensor"),
        P(),
        P(None, "tensor"),
        P(None, None, "tensor"),
        P("tensor", None),
        P("dp", "tensor", None, None),
        P("dp", "tensor", None, None),
    )
    out_specs = P("dp", "tensor")
    return jax.shard_map(shards, mesh=mesh, in_specs=in_specs, out_specs=out_specs, check_vma=False)
```

```python
import functools
import math

import jax
import jax.numpy as jnp
from jax import lax
from jax.experimental import pallas as pl
from jax.experimental.pallas import tpu as pltpu
from jax.sharding import PartitionSpec as P

EPS = 1e-05
NEG = -1e30
THETA = 500000.0
MESH = pl.DeviceIdType.MESH
VMEM_BYTES = 67043328


def layer_kernel(
    n_dp,
    n_t,
    capacity,
    ids_hbm,
    anc_hbm,
    len_hbm,
    gain_hbm,
    table_hbm,
    wq_hbm,
    wkv_hbm,
    wout_hbm,
    kc_hbm,
    vc_hbm,
    out_ref,
    ids_v,
    codes_v,
    codes_s,
    anc_v,
    len_s,
    gain_v,
    cos_v,
    sin_v,
    place_v,
    table_v,
    group_v,
    wq_v,
    wkv_v,
    wout_v,
    kc_v,
    vc_v,
    slot_send,
    slot_recv,
    ss_send,
    ss_recv,
    sst_send,
    sst_recv,
    emb_all,
    ctx_v,
    rs1_send,
    rs1_recv,
    rs2_send,
    rs2_recv,
    small_sem,
    table_sem,
    w_sem,
    wout_sem,
    ids_ssem,
    ids_rsem,
    row_ssem,
    row_rsem,
    ss_ssem,
    ss_rsem,
    sst_ssem,
    sst_rsem,
    ag_ssem,
    ag_rsem,
    fw_ssem,
    rs1_ssem,
    rs1_rsem,
    rs2_ssem,
    rs2_rsem,
):
    me = lax.axis_index("dp")
    t = lax.axis_index("tensor")
    chip = t // 2
    parity = t % 2
    partner = t + 1 - 2 * parity
    n_chip = n_t // 2
    nodes = ids_v.shape[-1]
    tiles, tile, width = table_v.shape
    vocab_rows = tiles * tile
    head_dim = kc_v.shape[-1]
    kv_local = kc_v.shape[0]
    heads = wq_v.shape[1] // head_dim
    groups = heads // kv_local
    slots = n_dp * capacity
    span = 4 * capacity * tile
    absent = 2 * capacity * tile
    n_part = emb_all.shape[0]
    part_width = width // n_part
    n_rs = rs1_send.shape[1]
    rs_width = width // n_rs

    def peer(m):
        return lax.rem(me + m, n_dp)

    def back(m):
        return (n_dp - m) % n_dp

    others = list(range(1, n_dp))

    barrier = pltpu.get_barrier_semaphore()
    for m in others:
        pl.semaphore_signal(barrier, inc=1, device_id={"dp": peer(m)}, device_id_type=MESH)
    for k in range(1, n_t):
        pl.semaphore_signal(
            barrier, inc=1, device_id={"tensor": lax.rem(t + k, n_t)}, device_id_type=MESH
        )
    small_copies = [
        pltpu.make_async_copy(ids_hbm, ids_v, small_sem.at[0]),
        pltpu.make_async_copy(anc_hbm.at[0], anc_v, small_sem.at[1]),
        pltpu.make_async_copy(len_hbm, len_s, small_sem.at[2]),
        pltpu.make_async_copy(gain_hbm, gain_v, small_sem.at[3]),
    ]
    for copy in small_copies:
        copy.start()
    n_tab = table_sem.shape[0]
    tab_step = tiles // n_tab
    table_copies = [
        pltpu.make_async_copy(
            table_hbm.at[pl.ds(i * tab_step, tab_step)],
            table_v.at[pl.ds(i * tab_step, tab_step)],
            table_sem.at[i],
        )
        for i in range(n_tab)
    ]
    for copy in table_copies:
        copy.start()
    small_copies[0].wait()
    sub = lax.broadcasted_iota(jnp.int32, (nodes, nodes), 0)
    lane = lax.broadcasted_iota(jnp.int32, (nodes, nodes), 1)
    ids_row = ids_v[...]
    ids = jnp.sum(jnp.where(sub == lane, ids_row, 0), axis=1, keepdims=True)
    owner = ids // vocab_rows
    alike = (owner == ids_row // vocab_rows) & (lane < sub)
    rank = jnp.sum(jnp.where(alike, 1, 0), axis=1, keepdims=True)
    node_slot = lax.rem(owner - me + n_dp, n_dp) * capacity + rank
    slot_index = lax.broadcasted_iota(jnp.int32, (nodes, slots), 1)
    placed = (node_slot == slot_index) & (rank < capacity)
    place_v[...] = jnp.where(placed, 1.0, 0.0)
    offset = ids - owner * vocab_rows
    code = (offset // tile) * span + lax.rem(offset, tile)
    codes_v[...] = jnp.sum(jnp.where(placed, code - absent, 0), axis=0, keepdims=True) + absent
    own_codes = pltpu.make_async_copy(codes_v, codes_s.at[0], small_sem.at[4])
    own_codes.start()
    pl.semaphore_wait(barrier, n_dp + n_t - 2)

    def dp_copy(src, dst, ssem, rsem, m):
        return pltpu.make_async_remote_copy(
            src_ref=src,
            dst_ref=dst,
            send_sem=ssem,
            recv_sem=rsem,
            device_id={"dp": peer(m)},
            device_id_type=MESH,
        )

    def t_copy(src, dst, ssem, rsem, target):
        return pltpu.make_async_remote_copy(
            src_ref=src,
            dst_ref=dst,
            send_sem=ssem,
            recv_sem=rsem,
            device_id={"tensor": target},
            device_id_type=MESH,
        )

    ids_copies = [
        dp_copy(codes_v, codes_s.at[back(m)], ids_ssem.at[m], ids_rsem.at[back(m)], m)
        for m in others
    ]
    for copy in ids_copies:
        copy.start()

    for copy in small_copies[1:]:
        copy.wait()
    live_slots = len_s[0]
    depth = jnp.sum(anc_v[...].astype(jnp.float32), axis=1, keepdims=True)
    positions = depth + (live_slots - 1).astype(jnp.float32)
    half_dim = head_dim // 2
    lanes = lax.broadcasted_iota(jnp.int32, (1, head_dim), 1)
    freq_index = jnp.where(lanes < half_dim, lanes, lanes - half_dim).astype(jnp.float32)
    angles = positions * jnp.exp(freq_index * (-2.0 * math.log(THETA) / head_dim))
    cosine = jnp.cos(angles)
    sine = jnp.where(lanes < half_dim, -jnp.sin(angles), jnp.sin(angles))
    cos_v[...] = cosine
    sin_v[...] = sine

    for copy in table_copies:
        copy.wait()

    w_copies = [
        pltpu.make_async_copy(wq_hbm, wq_v, w_sem.at[0]),
        pltpu.make_async_copy(wkv_hbm, wkv_v, w_sem.at[1]),
        pltpu.make_async_copy(kc_hbm.at[0], kc_v, w_sem.at[2]),
        pltpu.make_async_copy(vc_hbm.at[0], vc_v, w_sem.at[3]),
    ]
    wout_copies = []
    for k in list(range(1, n_chip)) + [0]:
        target_chip = lax.rem(chip + k, n_chip)
        for which in range(2):
            chunk = 2 * target_chip + (parity if which else 1 - parity)
            start = pl.multiple_of(chunk * width, width)
            wout_copies.append(
                pltpu.make_async_copy(
                    wout_hbm.at[:, pl.ds(start, width)],
                    wout_v.at[2 * k + which],
                    wout_sem.at[2 * k + which],
                )
            )
    for copy in w_copies + wout_copies:
        copy.start()

    own_codes.wait()
    for copy in ids_copies:
        copy.wait_recv()
    row_copies = []
    ss_copies = []
    block_sub = lax.broadcasted_iota(jnp.int32, (capacity, 128), 0)
    block_lane = lax.broadcasted_iota(jnp.int32, (capacity, 128), 1)
    squares = [None] * n_dp
    n_batch = 2

    def send_row(q, m):
        copy = dp_copy(
            slot_send.at[q, m],
            slot_recv.at[q, back(m)],
            row_ssem.at[q, m],
            row_rsem.at[q, back(m)],
            m,
        )
        copy.start()
        row_copies.append(copy)

    def look_up(m):
        target = jnp.full((capacity, 128), -1, jnp.int32)
        for i in range(capacity):
            code = codes_s[m, 0, back(m) * capacity + i]
            group = lax.div(code, span)
            row = (m * capacity + i) * tile
            group_v[row : row + tile, :] = table_v[group]
            target = jnp.where(block_sub == i, i * tile + code - group * span, target)
        pick = jnp.concatenate(
            [
                (block_lane + h == target).astype(jnp.float32).astype(jnp.bfloat16)
                for h in range(0, capacity * tile, 128)
            ],
            axis=1,
        )
        start = m * capacity * tile
        rows = jnp.dot(
            pick,
            group_v[start : start + capacity * tile, :],
            preferred_element_type=jnp.float32,
        )
        squares[m] = jnp.sum(rows * rows, axis=1, keepdims=True)
        for q in range(n_part):
            packed = rows[:, q * part_width : (q + 1) * part_width].astype(jnp.bfloat16)
            if m:
                slot_send[q, m] = packed
            else:
                slot_recv[q, 0] = packed

    batch = n_dp // n_batch
    order = others + [0]
    for first in range(0, n_dp, batch):
        for m in order[first : first + batch]:
            look_up(m)
        for m in order[first : first + batch]:
            if m:
                send_row(0, m)
    ordered = jnp.concatenate([squares[back(m)] for m in range(n_dp)], axis=0)
    row = jnp.broadcast_to(ordered, (slots, 128)).T[0:1]
    ss_send[...] = row
    ss_recv[0] = row
    for m in others:
        copy = dp_copy(ss_send, ss_recv.at[back(m)], ss_ssem.at[m], ss_rsem.at[back(m)], m)
        copy.start()
        ss_copies.append(copy)
    for q in range(1, n_part):
        for m in others:
            send_row(q, m)

    def ag_copy(q, origin, ssem, target):
        return t_copy(
            emb_all.at[q, origin], emb_all.at[q, origin], ssem, ag_rsem.at[q, origin], target
        )

    ag_copies = []
    fw_copies = []
    sst_copies = []

    def forward(q):
        for k in range(1, n_chip):
            origin = lax.rem(t - 2 * k + n_t, n_t)
            copy = ag_copy(q, origin, fw_ssem.at[q, k], partner)
            copy.wait_recv()
            copy.start()
            fw_copies.append(copy)

    def gathered(q):
        ag_copy(q, partner, ag_ssem.at[q, 0], partner).wait_recv()
        for k in range(1, n_chip):
            origin = lax.rem(partner - 2 * k + n_t, n_t)
            ag_copy(q, origin, ag_ssem.at[q, 0], partner).wait_recv()

    place = place_v[...].astype(jnp.bfloat16)
    slot_lane = lax.broadcasted_iota(jnp.int32, (1, slots), 1) // capacity
    for q in range(n_part):
        if q == n_part - 1:
            row = jnp.zeros((1, slots), jnp.float32)
            for m in range(n_dp):
                if m:
                    dp_copy(ss_send, ss_recv.at[m], ss_ssem.at[m], ss_rsem.at[m], m).wait_recv()
                row = jnp.where(slot_lane == m, ss_recv[m], row)
            sst_send[...] = row
            for k in range(1, n_t):
                copy = t_copy(
                    sst_send,
                    sst_recv.at[n_t - k],
                    sst_ssem.at[k],
                    sst_rsem.at[n_t - k],
                    lax.rem(t + k, n_t),
                )
                copy.start()
                sst_copies.append(copy)
        for m in range(1, n_dp):
            dp_copy(
                slot_send.at[q, m], slot_recv.at[q, m], row_ssem.at[q, m], row_rsem.at[q, m], m
            ).wait_recv()
        embedded = jnp.dot(
            place, slot_recv[q].reshape(slots, part_width), preferred_element_type=jnp.float32
        )
        emb_all[q, t] = embedded.astype(jnp.bfloat16)
        for k in list(range(1, n_chip)) + [0]:
            copy = ag_copy(q, t, ag_ssem.at[q, k], lax.rem(t + 2 * k, n_t) if k else partner)
            copy.start()
            ag_copies.append(copy)
        if q:
            forward(q - 1)

    total_row = sst_send[...]
    for k in range(1, n_t):
        t_copy(sst_send, sst_recv.at[k], sst_ssem.at[k], sst_rsem.at[k], partner).wait_recv()
        total_row = total_row + sst_recv[k]
    node_squares = jnp.sum(place_v[...] * total_row, axis=1, keepdims=True)
    inv_rms = lax.rsqrt(node_squares / (n_t * width) + EPS)
    for copy in w_copies:
        copy.wait()

    def project(first, last, sums):
        queries, keys, values = sums
        for j in range(n_t):
            start = j * width + first * part_width
            span = slice(start, start + (last - first) * part_width)
            gain = gain_v[span].astype(jnp.float32)[None, :]
            parts = [emb_all[q, j] for q in range(first, last)]
            features = jnp.concatenate(parts, axis=1) if len(parts) > 1 else parts[0]
            normed = (features.astype(jnp.float32) * inv_rms * gain).astype(jnp.bfloat16)
            queries = queries + jnp.dot(
                normed, wq_v[span, :], preferred_element_type=jnp.float32
            )
            keys = keys + jnp.dot(normed, wkv_v[0, span, :], preferred_element_type=jnp.float32)
            values = values + jnp.dot(
                normed, wkv_v[1, span, :], preferred_element_type=jnp.float32
            )
        return queries, keys, values

    sums = (
        jnp.zeros((nodes, wq_v.shape[1]), jnp.float32),
        jnp.zeros((nodes, wkv_v.shape[2]), jnp.float32),
        jnp.zeros((nodes, wkv_v.shape[2]), jnp.float32),
    )
    if n_part > 1:
        for q in range(n_part - 1):
            gathered(q)
        sums = project(0, n_part - 1, sums)
    forward(n_part - 1)
    gathered(n_part - 1)
    queries, keys_raw, values_raw = project(n_part - 1, n_part, sums)
    values_new = values_raw.astype(jnp.bfloat16)
    cosine = cos_v[...]
    sine = sin_v[...]

    def rotary(values):
        return (values * cosine + pltpu.roll(values, head_dim // 2, 1) * sine).astype(jnp.bfloat16)

    scale = head_dim ** (-0.5)
    live = lax.broadcasted_iota(jnp.int32, (1, kc_v.shape[1]), 1) < live_slots
    tree = jnp.concatenate([anc_v[...]] * groups, axis=0) > 0
    contract = (((1,), (1,)), ((), ()))
    for kv in range(kv_local):
        cols = slice(kv * head_dim, (kv + 1) * head_dim)
        query = jnp.concatenate(
            [
                rotary(queries[:, h * head_dim : (h + 1) * head_dim])
                for h in range(kv * groups, (kv + 1) * groups)
            ],
            axis=0,
        )
        key_tree = rotary(keys_raw[:, cols])
        cache_scores = (
            lax.dot_general(query, kc_v[kv], contract, preferred_element_type=jnp.float32) * scale
        )
        cache_scores = jnp.where(live, cache_scores, NEG)
        tree_scores = (
            lax.dot_general(query, key_tree, contract, preferred_element_type=jnp.float32) * scale
        )
        tree_scores = jnp.where(tree, tree_scores, NEG)
        top = jnp.maximum(
            jnp.max(cache_scores, axis=1, keepdims=True),
            jnp.max(tree_scores, axis=1, keepdims=True),
        )
        cache_exp = jnp.exp(cache_scores - top)
        tree_exp = jnp.exp(tree_scores - top)
        denominator = jnp.sum(cache_exp, axis=1, keepdims=True) + jnp.sum(
            tree_exp, axis=1, keepdims=True
        )
        weighted = jnp.dot(
            tree_exp.astype(jnp.bfloat16), values_new[:, cols], preferred_element_type=jnp.float32
        ) + jnp.dot(cache_exp.astype(jnp.bfloat16), vc_v[kv], preferred_element_type=jnp.float32)
        context = (weighted / denominator).astype(jnp.bfloat16)
        for g in range(groups):
            h = kv * groups + g
            ctx_v[:, h * head_dim : (h + 1) * head_dim] = context[g * nodes : (g + 1) * nodes]

    for copy in wout_copies:
        copy.wait()
    contexts = ctx_v[...]
    rs1_copies = {}
    rs2_copies = {}

    half = contexts.shape[1] // 2

    def out_part(block, c):
        cols = slice(c * rs_width, (c + 1) * rs_width)
        return jnp.dot(
            contexts[:, :half], wout_v[block, :half, cols], preferred_element_type=jnp.float32
        ) + jnp.dot(
            contexts[:, half:], wout_v[block, half:, cols], preferred_element_type=jnp.float32
        )

    def to_partner(k):
        for c in range(n_rs):
            rs1_send[k, c] = out_part(2 * k, c).astype(jnp.bfloat16)
            rs1_copies[k, c] = t_copy(
                rs1_send.at[k, c], rs1_recv.at[k, c], rs1_ssem.at[k, c], rs1_rsem.at[k, c], partner
            )
            rs1_copies[k, c].start()

    for k in range(1, n_chip):
        to_partner(k)
    for k in range(1, n_chip):
        for c in range(n_rs):
            part = out_part(2 * k + 1, c)
            rs1_copies[k, c].wait_recv()
            rs2_send[k, c] = (part + rs1_recv[k, c].astype(jnp.float32)).astype(jnp.bfloat16)
            rs2_copies[k, c] = t_copy(
                rs2_send.at[k, c],
                rs2_recv.at[k, c],
                rs2_ssem.at[k, c],
                rs2_rsem.at[k, c],
                lax.rem(t + 2 * k, n_t),
            )
            rs2_copies[k, c].start()
    to_partner(0)
    own = jnp.concatenate([emb_all[q, t].astype(jnp.float32) for q in range(n_part)], axis=1)
    sums = []
    for c in range(n_rs):
        part = out_part(1, c)
        rs1_copies[0, c].wait_recv()
        part = part + rs1_recv[0, c].astype(jnp.float32)
        sums.append(part + own[:, c * rs_width : (c + 1) * rs_width])
    for c in range(n_rs):
        total = sums[c]
        for k in range(1, n_chip):
            rs2_copies[k, c].wait_recv()
            total = total + rs2_recv[k, c].astype(jnp.float32)
        out_ref[:, c * rs_width : (c + 1) * rs_width] = total.astype(out_ref.dtype)
    for copy in (
        ids_copies
        + row_copies
        + ss_copies
        + ag_copies
        + sst_copies
        + fw_copies
        + list(rs1_copies.values())
        + list(rs2_copies.values())
    ):
        copy.wait_send()


def shards(tree_ids, ancestors, lengths, table, gain, w_query, w_kv, w_out, key_cache, value_cache):
    n_dp = lax.axis_size("dp")
    n_t = lax.axis_size("tensor")
    n_chip = n_t // 2
    row_count, nodes = tree_ids.shape
    vocab_rows, width = table.shape
    head_dim = key_cache.shape[3]
    capacity = 2 * ((row_count * nodes + n_dp - 1) // n_dp)
    capacity = 16 * ((capacity + 15) // 16)
    bf16, f32 = jnp.bfloat16, jnp.float32
    n_tab = 4
    tile = 16
    n_part = 2
    n_rs = 2
    part_width = width // n_part
    rs_width = width // n_rs
    slots = n_dp * capacity
    sems = pltpu.SemaphoreType.DMA
    hbm = pl.BlockSpec(memory_space=pl.ANY)
    return pl.pallas_call(
        functools.partial(layer_kernel, n_dp, n_t, capacity),
        out_shape=pltpu.VMEM((nodes, width), bf16),
        in_specs=[hbm] * 2 + [pl.BlockSpec(memory_space=pltpu.HBM)] + [hbm] * 7,
        out_specs=pl.BlockSpec(memory_space=pltpu.VMEM),
        scratch_shapes=[
            pltpu.VMEM((1, nodes), jnp.int32),
            pltpu.VMEM((1, slots), jnp.int32),
            pltpu.SMEM((n_dp, 1, slots), jnp.int32),
            pltpu.VMEM((nodes, nodes), jnp.int32),
            pltpu.SMEM(lengths.shape, jnp.int32),
            pltpu.VMEM(gain.shape, bf16),
            pltpu.VMEM((nodes, head_dim), f32),
            pltpu.VMEM((nodes, head_dim), f32),
            pltpu.VMEM((nodes, slots), f32),
            pltpu.VMEM((vocab_rows // tile, tile, width), bf16),
            pltpu.VMEM((slots * tile, width), bf16),
            pltpu.VMEM(w_query.shape, bf16),
            pltpu.VMEM(w_kv.shape, bf16),
            pltpu.VMEM((n_t, w_out.shape[0], width), bf16),
            pltpu.VMEM(key_cache.shape[1:], bf16),
            pltpu.VMEM(value_cache.shape[1:], bf16),
            pltpu.VMEM((n_part, n_dp, capacity, part_width), bf16),
            pltpu.VMEM((n_part, n_dp, capacity, part_width), bf16),
            pltpu.VMEM((1, slots), f32),
            pltpu.VMEM((n_dp, 1, slots), f32),
            pltpu.VMEM((1, slots), f32),
            pltpu.VMEM((n_t, 1, slots), f32),
            pltpu.VMEM((n_part, n_t, nodes, part_width), bf16),
            pltpu.VMEM((nodes, w_query.shape[1]), bf16),
            pltpu.VMEM((n_chip, n_rs, nodes, rs_width), bf16),
            pltpu.VMEM((n_chip, n_rs, nodes, rs_width), bf16),
            pltpu.VMEM((n_chip, n_rs, nodes, rs_width), bf16),
            pltpu.VMEM((n_chip, n_rs, nodes, rs_width), bf16),
            sems((5,)),
            sems((n_tab,)),
            sems((4,)),
            sems((n_t,)),
            sems((n_dp,)),
            sems((n_dp,)),
            sems((n_part, n_dp)),
            sems((n_part, n_dp)),
            sems((n_dp,)),
            sems((n_dp,)),
            sems((n_t,)),
            sems((n_t,)),
            sems((n_part, n_chip)),
            sems((n_part, n_t)),
            sems((n_part, n_chip)),
            sems((n_chip, n_rs)),
            sems((n_chip, n_rs)),
            sems((n_chip, n_rs)),
            sems((n_chip, n_rs)),
        ],
        compiler_params=pltpu.CompilerParams(
            collective_id=0,
            has_side_effects=True,
            vmem_limit_bytes=VMEM_BYTES - 2 * nodes * width,
        ),
    )(
        tree_ids,
        ancestors,
        lengths,
        gain,
        table.reshape(vocab_rows // tile, tile, width),
        w_query,
        w_kv,
        w_out,
        key_cache,
        value_cache,
    )


def solution(mesh):
    in_specs = (
        P("dp", None),
        P("dp", None, None),
        P("dp"),
        P("dp", "tensor"),
        P(),
        P(None, "tensor"),
        P(None, None, "tensor"),
        P("tensor", None),
        P("dp", "tensor", None, None),
        P("dp", "tensor", None, None),
    )
    out_specs = P("dp", "tensor")
    return jax.shard_map(shards, mesh=mesh, in_specs=in_specs, out_specs=out_specs, check_vma=False)
```

```python
import functools
import math

import jax
import jax.numpy as jnp
from jax import lax
from jax.experimental import pallas as pl
from jax.experimental.pallas import tpu as pltpu
from jax.sharding import PartitionSpec as P

EPS = 1e-05
NEG = -1e30
THETA = 500000.0
MESH = pl.DeviceIdType.MESH
VMEM_BYTES = 67043328


def layer_kernel(
    n_dp,
    n_t,
    capacity,
    ids_hbm,
    anc_hbm,
    len_hbm,
    gain_hbm,
    table_hbm,
    wq_hbm,
    wkv_hbm,
    wout_hbm,
    kc_hbm,
    vc_hbm,
    out_ref,
    ids_v,
    codes_v,
    codes_s,
    anc_v,
    len_s,
    gain_v,
    cos_v,
    sin_v,
    place_v,
    table_v,
    group_v,
    wq_v,
    wkv_v,
    wout_v,
    kc_v,
    vc_v,
    slot_send,
    slot_recv,
    ss_send,
    ss_recv,
    sst_send,
    sst_recv,
    emb_all,
    ctx_v,
    rs1_send,
    rs1_recv,
    rs2_send,
    rs2_recv,
    small_sem,
    table_sem,
    w_sem,
    wout_sem,
    ids_ssem,
    ids_rsem,
    row_ssem,
    row_rsem,
    ss_ssem,
    ss_rsem,
    sst_ssem,
    sst_rsem,
    ag_ssem,
    ag_rsem,
    fw_ssem,
    rs1_ssem,
    rs1_rsem,
    rs2_ssem,
    rs2_rsem,
):
    me = lax.axis_index("dp")
    t = lax.axis_index("tensor")
    chip = t // 2
    parity = t % 2
    partner = t + 1 - 2 * parity
    n_chip = n_t // 2
    nodes = ids_v.shape[-1]
    tiles, tile, width = table_v.shape
    vocab_rows = tiles * tile
    head_dim = kc_v.shape[-1]
    kv_local = kc_v.shape[0]
    heads = wq_v.shape[1] // head_dim
    groups = heads // kv_local
    slots = n_dp * capacity
    span = 4 * capacity * tile
    absent = 2 * capacity * tile
    n_part = emb_all.shape[0]
    part_width = width // n_part
    n_rs = rs1_send.shape[1]
    rs_width = width // n_rs

    def peer(m):
        return lax.rem(me + m, n_dp)

    def back(m):
        return (n_dp - m) % n_dp

    others = list(range(1, n_dp))

    barrier = pltpu.get_barrier_semaphore()
    for m in others:
        pl.semaphore_signal(barrier, inc=1, device_id={"dp": peer(m)}, device_id_type=MESH)
    for k in range(1, n_t):
        pl.semaphore_signal(
            barrier, inc=1, device_id={"tensor": lax.rem(t + k, n_t)}, device_id_type=MESH
        )
    small_copies = [
        pltpu.make_async_copy(ids_hbm, ids_v, small_sem.at[0]),
        pltpu.make_async_copy(anc_hbm.at[0], anc_v, small_sem.at[1]),
        pltpu.make_async_copy(len_hbm, len_s, small_sem.at[2]),
        pltpu.make_async_copy(gain_hbm, gain_v, small_sem.at[3]),
    ]
    for copy in small_copies:
        copy.start()
    n_tab = table_sem.shape[0]
    tab_step = tiles // n_tab
    table_copies = [
        pltpu.make_async_copy(
            table_hbm.at[pl.ds(i * tab_step, tab_step)],
            table_v.at[pl.ds(i * tab_step, tab_step)],
            table_sem.at[i],
        )
        for i in range(n_tab)
    ]
    for copy in table_copies:
        copy.start()
    small_copies[0].wait()
    sub = lax.broadcasted_iota(jnp.int32, (nodes, nodes), 0)
    lane = lax.broadcasted_iota(jnp.int32, (nodes, nodes), 1)
    ids_row = ids_v[...]
    ids = jnp.sum(jnp.where(sub == lane, ids_row, 0), axis=1, keepdims=True)
    owner = ids // vocab_rows
    alike = (owner == ids_row // vocab_rows) & (lane < sub)
    rank = jnp.sum(jnp.where(alike, 1, 0), axis=1, keepdims=True)
    node_slot = lax.rem(owner - me + n_dp, n_dp) * capacity + rank
    slot_index = lax.broadcasted_iota(jnp.int32, (nodes, slots), 1)
    placed = (node_slot == slot_index) & (rank < capacity)
    place_v[...] = jnp.where(placed, 1.0, 0.0)
    offset = ids - owner * vocab_rows
    code = (offset // tile) * span + lax.rem(offset, tile)
    codes_v[...] = jnp.sum(jnp.where(placed, code - absent, 0), axis=0, keepdims=True) + absent
    own_codes = pltpu.make_async_copy(codes_v, codes_s.at[0], small_sem.at[4])
    own_codes.start()
    pl.semaphore_wait(barrier, n_dp + n_t - 2)

    def dp_copy(src, dst, ssem, rsem, m):
        return pltpu.make_async_remote_copy(
            src_ref=src,
            dst_ref=dst,
            send_sem=ssem,
            recv_sem=rsem,
            device_id={"dp": peer(m)},
            device_id_type=MESH,
        )

    def t_copy(src, dst, ssem, rsem, target):
        return pltpu.make_async_remote_copy(
            src_ref=src,
            dst_ref=dst,
            send_sem=ssem,
            recv_sem=rsem,
            device_id={"tensor": target},
            device_id_type=MESH,
        )

    ids_copies = [
        dp_copy(codes_v, codes_s.at[back(m)], ids_ssem.at[m], ids_rsem.at[back(m)], m)
        for m in others
    ]
    for copy in ids_copies:
        copy.start()

    for copy in small_copies[1:]:
        copy.wait()
    live_slots = len_s[0]
    depth = jnp.sum(anc_v[...].astype(jnp.float32), axis=1, keepdims=True)
    positions = depth + (live_slots - 1).astype(jnp.float32)
    half_dim = head_dim // 2
    lanes = lax.broadcasted_iota(jnp.int32, (1, head_dim), 1)
    freq_index = jnp.where(lanes < half_dim, lanes, lanes - half_dim).astype(jnp.float32)
    angles = positions * jnp.exp(freq_index * (-2.0 * math.log(THETA) / head_dim))
    cosine = jnp.cos(angles)
    sine = jnp.where(lanes < half_dim, -jnp.sin(angles), jnp.sin(angles))
    cos_v[...] = cosine
    sin_v[...] = sine

    for copy in table_copies:
        copy.wait()

    w_copies = [
        pltpu.make_async_copy(wq_hbm, wq_v, w_sem.at[0]),
        pltpu.make_async_copy(wkv_hbm, wkv_v, w_sem.at[1]),
        pltpu.make_async_copy(kc_hbm.at[0], kc_v, w_sem.at[2]),
        pltpu.make_async_copy(vc_hbm.at[0], vc_v, w_sem.at[3]),
    ]
    wout_copies = []
    for k in list(range(1, n_chip)) + [0]:
        target_chip = lax.rem(chip + k, n_chip)
        for which in range(2):
            chunk = 2 * target_chip + (parity if which else 1 - parity)
            start = pl.multiple_of(chunk * width, width)
            wout_copies.append(
                pltpu.make_async_copy(
                    wout_hbm.at[:, pl.ds(start, width)],
                    wout_v.at[2 * k + which],
                    wout_sem.at[2 * k + which],
                )
            )
    for copy in w_copies + wout_copies:
        copy.start()

    own_codes.wait()
    for copy in ids_copies:
        copy.wait_recv()
    row_copies = []
    ss_copies = []
    block_sub = lax.broadcasted_iota(jnp.int32, (capacity, 128), 0)
    block_lane = lax.broadcasted_iota(jnp.int32, (capacity, 128), 1)
    squares = [None] * n_dp
    n_batch = 2

    def send_row(q, m):
        copy = dp_copy(
            slot_send.at[q, m],
            slot_recv.at[q, back(m)],
            row_ssem.at[q, m],
            row_rsem.at[q, back(m)],
            m,
        )
        copy.start()
        row_copies.append(copy)

    def look_up(m):
        target = jnp.full((capacity, 128), -1, jnp.int32)
        for i in range(capacity):
            code = codes_s[m, 0, back(m) * capacity + i]
            group = lax.div(code, span)
            row = (m * capacity + i) * tile
            group_v[row : row + tile, :] = table_v[group]
            target = jnp.where(block_sub == i, i * tile + code - group * span, target)
        pick = jnp.concatenate(
            [
                (block_lane + h == target).astype(jnp.float32).astype(jnp.bfloat16)
                for h in range(0, capacity * tile, 128)
            ],
            axis=1,
        )
        start = m * capacity * tile
        rows = jnp.dot(
            pick,
            group_v[start : start + capacity * tile, :],
            preferred_element_type=jnp.float32,
        )
        squares[m] = jnp.sum(rows * rows, axis=1, keepdims=True)
        for q in range(n_part):
            packed = rows[:, q * part_width : (q + 1) * part_width].astype(jnp.bfloat16)
            if m:
                slot_send[q, m] = packed
            else:
                slot_recv[q, 0] = packed

    batch = n_dp // n_batch
    order = others + [0]
    for first in range(0, n_dp, batch):
        for m in order[first : first + batch]:
            look_up(m)
        for m in order[first : first + batch]:
            if m:
                send_row(0, m)
    ordered = jnp.concatenate([squares[back(m)] for m in range(n_dp)], axis=0)
    row = jnp.broadcast_to(ordered, (slots, 128)).T[0:1]
    ss_send[...] = row
    ss_recv[0] = row
    for m in others:
        copy = dp_copy(ss_send, ss_recv.at[back(m)], ss_ssem.at[m], ss_rsem.at[back(m)], m)
        copy.start()
        ss_copies.append(copy)
    for q in range(1, n_part):
        for m in others:
            send_row(q, m)

    def ag_copy(q, origin, ssem, target):
        return t_copy(
            emb_all.at[q, origin], emb_all.at[q, origin], ssem, ag_rsem.at[q, origin], target
        )

    ag_copies = []
    fw_copies = [
        ag_copy(q, t, fw_ssem.at[q, k], partner) for q in range(n_part) for k in range(1, n_chip)
    ]
    sst_copies = []

    def forward(q):
        for k in range(1, n_chip):
            origin = lax.rem(t - 2 * k + n_t, n_t)
            copy = ag_copy(q, origin, fw_ssem.at[q, k], partner)
            copy.wait_recv()
            copy.start()

    def gathered(q):
        ag_copy(q, partner, ag_ssem.at[q, 0], partner).wait_recv()
        for k in range(1, n_chip):
            origin = lax.rem(partner - 2 * k + n_t, n_t)
            ag_copy(q, origin, ag_ssem.at[q, 0], partner).wait_recv()

    place = place_v[...].astype(jnp.bfloat16)
    slot_lane = lax.broadcasted_iota(jnp.int32, (1, slots), 1) // capacity
    for q in range(n_part):
        if q == n_part - 1:
            row = jnp.zeros((1, slots), jnp.float32)
            for m in range(n_dp):
                if m:
                    dp_copy(ss_send, ss_recv.at[m], ss_ssem.at[m], ss_rsem.at[m], m).wait_recv()
                row = jnp.where(slot_lane == m, ss_recv[m], row)
            sst_send[...] = row
            for k in range(1, n_t):
                copy = t_copy(
                    sst_send,
                    sst_recv.at[n_t - k],
                    sst_ssem.at[k],
                    sst_rsem.at[n_t - k],
                    lax.rem(t + k, n_t),
                )
                copy.start()
                sst_copies.append(copy)
        for m in range(1, n_dp):
            dp_copy(
                slot_send.at[q, m], slot_recv.at[q, m], row_ssem.at[q, m], row_rsem.at[q, m], m
            ).wait_recv()
        embedded = jnp.dot(
            place, slot_recv[q].reshape(slots, part_width), preferred_element_type=jnp.float32
        )
        emb_all[q, t] = embedded.astype(jnp.bfloat16)
        for k in list(range(1, n_chip)) + [0]:
            copy = ag_copy(q, t, ag_ssem.at[q, k], lax.rem(t + 2 * k, n_t) if k else partner)
            copy.start()
            ag_copies.append(copy)
        if q:
            forward(q - 1)

    @pl.when(parity == 1)
    def _():
        forward(n_part - 1)

    total_row = sst_send[...]
    for k in range(1, n_t):
        t_copy(sst_send, sst_recv.at[k], sst_ssem.at[k], sst_rsem.at[k], partner).wait_recv()
        total_row = total_row + sst_recv[k]
    node_squares = jnp.sum(place_v[...] * total_row, axis=1, keepdims=True)
    inv_rms = lax.rsqrt(node_squares / (n_t * width) + EPS)
    for copy in w_copies:
        copy.wait()

    def project(first, last, sums):
        queries, keys, values = sums
        for j in range(n_t):
            start = j * width + first * part_width
            span = slice(start, start + (last - first) * part_width)
            gain = gain_v[span].astype(jnp.float32)[None, :]
            parts = [emb_all[q, j] for q in range(first, last)]
            features = jnp.concatenate(parts, axis=1) if len(parts) > 1 else parts[0]
            normed = (features.astype(jnp.float32) * inv_rms * gain).astype(jnp.bfloat16)
            queries = queries + jnp.dot(
                normed, wq_v[span, :], preferred_element_type=jnp.float32
            )
            keys = keys + jnp.dot(normed, wkv_v[0, span, :], preferred_element_type=jnp.float32)
            values = values + jnp.dot(
                normed, wkv_v[1, span, :], preferred_element_type=jnp.float32
            )
        return queries, keys, values

    sums = (
        jnp.zeros((nodes, wq_v.shape[1]), jnp.float32),
        jnp.zeros((nodes, wkv_v.shape[2]), jnp.float32),
        jnp.zeros((nodes, wkv_v.shape[2]), jnp.float32),
    )
    if n_part > 1:
        for q in range(n_part - 1):
            gathered(q)
        sums = project(0, n_part - 1, sums)
    @pl.when(parity == 0)
    def _():
        forward(n_part - 1)

    gathered(n_part - 1)
    queries, keys_raw, values_raw = project(n_part - 1, n_part, sums)
    values_new = values_raw.astype(jnp.bfloat16)
    cosine = cos_v[...]
    sine = sin_v[...]

    def rotary(values):
        return (values * cosine + pltpu.roll(values, head_dim // 2, 1) * sine).astype(jnp.bfloat16)

    scale = head_dim ** (-0.5)
    live = lax.broadcasted_iota(jnp.int32, (1, kc_v.shape[1]), 1) < live_slots
    tree = jnp.concatenate([anc_v[...]] * groups, axis=0) > 0
    contract = (((1,), (1,)), ((), ()))
    for kv in range(kv_local):
        cols = slice(kv * head_dim, (kv + 1) * head_dim)
        query = jnp.concatenate(
            [
                rotary(queries[:, h * head_dim : (h + 1) * head_dim])
                for h in range(kv * groups, (kv + 1) * groups)
            ],
            axis=0,
        )
        key_tree = rotary(keys_raw[:, cols])
        cache_scores = (
            lax.dot_general(query, kc_v[kv], contract, preferred_element_type=jnp.float32) * scale
        )
        cache_scores = jnp.where(live, cache_scores, NEG)
        tree_scores = (
            lax.dot_general(query, key_tree, contract, preferred_element_type=jnp.float32) * scale
        )
        tree_scores = jnp.where(tree, tree_scores, NEG)
        top = jnp.maximum(
            jnp.max(cache_scores, axis=1, keepdims=True),
            jnp.max(tree_scores, axis=1, keepdims=True),
        )
        cache_exp = jnp.exp(cache_scores - top)
        tree_exp = jnp.exp(tree_scores - top)
        denominator = jnp.sum(cache_exp, axis=1, keepdims=True) + jnp.sum(
            tree_exp, axis=1, keepdims=True
        )
        weighted = jnp.dot(
            tree_exp.astype(jnp.bfloat16), values_new[:, cols], preferred_element_type=jnp.float32
        ) + jnp.dot(cache_exp.astype(jnp.bfloat16), vc_v[kv], preferred_element_type=jnp.float32)
        context = (weighted / denominator).astype(jnp.bfloat16)
        for g in range(groups):
            h = kv * groups + g
            ctx_v[:, h * head_dim : (h + 1) * head_dim] = context[g * nodes : (g + 1) * nodes]

    for copy in wout_copies:
        copy.wait()
    contexts = ctx_v[...]
    rs1_copies = {}
    rs2_copies = {}

    half = contexts.shape[1] // 2

    def out_part(block, c):
        cols = slice(c * rs_width, (c + 1) * rs_width)
        return jnp.dot(
            contexts[:, :half], wout_v[block, :half, cols], preferred_element_type=jnp.float32
        ) + jnp.dot(
            contexts[:, half:], wout_v[block, half:, cols], preferred_element_type=jnp.float32
        )

    def to_partner(k):
        for c in range(n_rs):
            rs1_send[k, c] = out_part(2 * k, c).astype(jnp.bfloat16)
            rs1_copies[k, c] = t_copy(
                rs1_send.at[k, c], rs1_recv.at[k, c], rs1_ssem.at[k, c], rs1_rsem.at[k, c], partner
            )
            rs1_copies[k, c].start()

    for k in range(1, n_chip):
        to_partner(k)
    for k in range(1, n_chip):
        for c in range(n_rs):
            part = out_part(2 * k + 1, c)
            rs1_copies[k, c].wait_recv()
            rs2_send[k, c] = (part + rs1_recv[k, c].astype(jnp.float32)).astype(jnp.bfloat16)
            rs2_copies[k, c] = t_copy(
                rs2_send.at[k, c],
                rs2_recv.at[k, c],
                rs2_ssem.at[k, c],
                rs2_rsem.at[k, c],
                lax.rem(t + 2 * k, n_t),
            )
            rs2_copies[k, c].start()
    to_partner(0)
    own = jnp.concatenate([emb_all[q, t].astype(jnp.float32) for q in range(n_part)], axis=1)
    sums = []
    for c in range(n_rs):
        part = out_part(1, c)
        rs1_copies[0, c].wait_recv()
        part = part + rs1_recv[0, c].astype(jnp.float32)
        sums.append(part + own[:, c * rs_width : (c + 1) * rs_width])
    for c in range(n_rs):
        total = sums[c]
        for k in range(1, n_chip):
            rs2_copies[k, c].wait_recv()
            total = total + rs2_recv[k, c].astype(jnp.float32)
        out_ref[:, c * rs_width : (c + 1) * rs_width] = total.astype(out_ref.dtype)
    for copy in (
        ids_copies
        + row_copies
        + ss_copies
        + ag_copies
        + sst_copies
        + fw_copies
        + list(rs1_copies.values())
        + list(rs2_copies.values())
    ):
        copy.wait_send()


def shards(tree_ids, ancestors, lengths, table, gain, w_query, w_kv, w_out, key_cache, value_cache):
    n_dp = lax.axis_size("dp")
    n_t = lax.axis_size("tensor")
    n_chip = n_t // 2
    row_count, nodes = tree_ids.shape
    vocab_rows, width = table.shape
    head_dim = key_cache.shape[3]
    capacity = 2 * ((row_count * nodes + n_dp - 1) // n_dp)
    capacity = 16 * ((capacity + 15) // 16)
    bf16, f32 = jnp.bfloat16, jnp.float32
    n_tab = 4
    tile = 16
    n_part = 2
    n_rs = 2
    part_width = width // n_part
    rs_width = width // n_rs
    slots = n_dp * capacity
    sems = pltpu.SemaphoreType.DMA
    hbm = pl.BlockSpec(memory_space=pl.ANY)
    return pl.pallas_call(
        functools.partial(layer_kernel, n_dp, n_t, capacity),
        out_shape=pltpu.VMEM((nodes, width), bf16),
        in_specs=[hbm] * 2 + [pl.BlockSpec(memory_space=pltpu.HBM)] + [hbm] * 7,
        out_specs=pl.BlockSpec(memory_space=pltpu.VMEM),
        scratch_shapes=[
            pltpu.VMEM((1, nodes), jnp.int32),
            pltpu.VMEM((1, slots), jnp.int32),
            pltpu.SMEM((n_dp, 1, slots), jnp.int32),
            pltpu.VMEM((nodes, nodes), jnp.int32),
            pltpu.SMEM(lengths.shape, jnp.int32),
            pltpu.VMEM(gain.shape, bf16),
            pltpu.VMEM((nodes, head_dim), f32),
            pltpu.VMEM((nodes, head_dim), f32),
            pltpu.VMEM((nodes, slots), f32),
            pltpu.VMEM((vocab_rows // tile, tile, width), bf16),
            pltpu.VMEM((slots * tile, width), bf16),
            pltpu.VMEM(w_query.shape, bf16),
            pltpu.VMEM(w_kv.shape, bf16),
            pltpu.VMEM((n_t, w_out.shape[0], width), bf16),
            pltpu.VMEM(key_cache.shape[1:], bf16),
            pltpu.VMEM(value_cache.shape[1:], bf16),
            pltpu.VMEM((n_part, n_dp, capacity, part_width), bf16),
            pltpu.VMEM((n_part, n_dp, capacity, part_width), bf16),
            pltpu.VMEM((1, slots), f32),
            pltpu.VMEM((n_dp, 1, slots), f32),
            pltpu.VMEM((1, slots), f32),
            pltpu.VMEM((n_t, 1, slots), f32),
            pltpu.VMEM((n_part, n_t, nodes, part_width), bf16),
            pltpu.VMEM((nodes, w_query.shape[1]), bf16),
            pltpu.VMEM((n_chip, n_rs, nodes, rs_width), bf16),
            pltpu.VMEM((n_chip, n_rs, nodes, rs_width), bf16),
            pltpu.VMEM((n_chip, n_rs, nodes, rs_width), bf16),
            pltpu.VMEM((n_chip, n_rs, nodes, rs_width), bf16),
            sems((5,)),
            sems((n_tab,)),
            sems((4,)),
            sems((n_t,)),
            sems((n_dp,)),
            sems((n_dp,)),
            sems((n_part, n_dp)),
            sems((n_part, n_dp)),
            sems((n_dp,)),
            sems((n_dp,)),
            sems((n_t,)),
            sems((n_t,)),
            sems((n_part, n_chip)),
            sems((n_part, n_t)),
            sems((n_part, n_chip)),
            sems((n_chip, n_rs)),
            sems((n_chip, n_rs)),
            sems((n_chip, n_rs)),
            sems((n_chip, n_rs)),
        ],
        compiler_params=pltpu.CompilerParams(
            collective_id=0,
            has_side_effects=True,
            vmem_limit_bytes=VMEM_BYTES - 2 * nodes * width,
        ),
    )(
        tree_ids,
        ancestors,
        lengths,
        gain,
        table.reshape(vocab_rows // tile, tile, width),
        w_query,
        w_kv,
        w_out,
        key_cache,
        value_cache,
    )


def solution(mesh):
    in_specs = (
        P("dp", None),
        P("dp", None, None),
        P("dp"),
        P("dp", "tensor"),
        P(),
        P(None, "tensor"),
        P(None, None, "tensor"),
        P("tensor", None),
        P("dp", "tensor", None, None),
        P("dp", "tensor", None, None),
    )
    out_specs = P("dp", "tensor")
    return jax.shard_map(shards, mesh=mesh, in_specs=in_specs, out_specs=out_specs, check_vma=False)
```
